32 devices in a mesh: head: 4 (over y, core), blk: 8 (over z, x).
Axes of the slice: x: 2, y: 2, z: 4, core: 2. Of those that a mesh axis runs over, the one named last changes fastest.
Arguments:
- embedded: bfloat16 [4096, 2048], P(('blk', 'head')), may hold values from -10.5 to 10.5
- cotangent: bfloat16 [4096, 2048], P(('blk', 'head')), may hold values from -6 to 6
- doc_lengths: int32 [8], replicated, may hold values from 1 to 1024, 4096 in all
- emb_gain: float32 [2048], replicated, may hold values from 0.25 to 1.75
- emb_bias: float32 [2048], replicated, may hold values from -3 to 3
- attn_gain: float32 [2, 2048], replicated, may hold values from 0.25 to 1.75
- attn_bias: float32 [2, 2048], replicated, may hold values from -3 to 3
- qkv_weight: bfloat16 [2, 2048, 6144], P(None, 'blk', 'head'), may hold values from -0.125 to 0.125
- qv_bias: float32 [2, 16, 2, 128], replicated, may hold values from -4 to 4
- out_weight: bfloat16 [2, 2048, 2048], P(None, 'head', 'blk'), may hold values from -0.5 to 0.5
- out_bias: float32 [2, 2048], replicated, may hold values from -4 to 4
- ffn_gain: float32 [2, 2048], replicated, may hold values from 0.25 to 1.75
- ffn_bias: float32 [2, 2048], replicated, may hold values from -3 to 3
- up_weight: bfloat16 [2, 2048, 8192], P(None, 'blk', 'head'), may hold values from -0.125 to 0.125
- up_bias: float32 [2, 8192], replicated, may hold values from -4 to 4
- down_weight: bfloat16 [2, 8192, 2048], P(None, 'head', 'blk'), may hold values from -0.0625 to 0.0625
- down_bias: float32 [2, 2048], replicated, may hold values from -4 to 4
Outputs:
- hidden_out: float32 [4096, 2048], P(('blk', 'head'))
- embedded_grad: float32 [4096, 2048], P(('blk', 'head'))
- emb_gain_grad: float32 [2048], replicated
- emb_bias_grad: float32 [2048], replicated
- attn_gain_grad: float32 [2, 2048], replicated
- attn_bias_grad: float32 [2, 2048], replicated
- qkv_weight_grad: float32 [2, 2048, 6144], P(None, 'blk', 'head')
- qv_bias_grad: float32 [2, 16, 2, 128], replicated
- out_weight_grad: float32 [2, 2048, 2048], P(None, 'head', 'blk')
- out_bias_grad: float32 [2, 2048], replicated
- ffn_gain_grad: float32 [2, 2048], replicated
- ffn_bias_grad: float32 [2, 2048], replicated
- up_weight_grad: float32 [2, 2048, 8192], P(None, 'blk', 'head')
- up_bias_grad: float32 [2, 8192], replicated
- down_weight_grad: float32 [2, 8192, 2048], P(None, 'head', 'blk')
- down_bias_grad: float32 [2, 2048], replicated
The draws below stay inside these ranges and needn't reach their ends.
Inputs may be any that keep to these rules, and one draw needn't show every extreme that they name: `doc_lengths`: lengths of the 8 documents laid end to end in the stream, summing to 4096; the longest is exactly 1024.
All inputs are finite; a program needn't handle non-finite values.
Results may differ from the reference program's by a relative error of at most 0.015.
Values may be sent and summed in bfloat16 or wider, within the bound.
A program may use at most 512 MiB of HBM per device.

```python
import math
import jax
import jax.numpy as jnp
import numpy as np
from jax import lax

D = 2048
H = 16
HD = 128
FF = 8192
LAYERS = 2
TOK_DEV = 128
TOKENS = 4096
DOC_MAX = 1024
NDOCS = 8
N_HEAD = 4


def draw_embedded(key, part):
    noise_key = jax.random.fold_in(key, 11)
    line_key = jax.random.fold_in(key, 12)
    phase_key = jax.random.fold_in(key, 13)
    positions = jnp.arange(TOKENS).astype(jnp.float32)
    period = 4.0 * TOK_DEV * N_HEAD
    phase_shift = jax.random.uniform(phase_key, (), jnp.float32, 0.0, 2.0 * math.pi)
    angle_now = 2.0 * math.pi * positions / period + phase_shift
    direction = jnp.clip(jax.random.normal(line_key, (D,), jnp.float32), -3.0, 3.0)
    rough_part = jnp.clip(jax.random.normal(noise_key, (TOKENS, D), jnp.float32), -6.0, 6.0)
    slow_wave = jnp.sin(angle_now)
    return (rough_part + 1.5 * slow_wave[:, None] * direction[None, :]).astype(jnp.bfloat16)


def steps_of(rng, shape, cuts, low, top_value):
    def one(axis_at, shards_of):
        heights = jax.random.uniform(jax.random.fold_in(jax.random.fold_in(rng, 6), axis_at), (shards_of,), jnp.float32, low / len(cuts), top_value / len(cuts))
        return jnp.repeat(jnp.exp(heights), shape[axis_at] // shards_of).reshape((-1,) + (1,) * (len(shape) - axis_at - 1))

    factor_of = one(*cuts[0])
    for cut in cuts[1:]:
        factor_of = factor_of * one(*cut)
    return factor_of


def split_up(number_of, total, most, skew):
    weights = [(1 << 20) // math.isqrt(rank ** skew) + 1 for rank in range(2, number_of + 1)]
    rest, holding = total - most - (number_of - 1), [1] * (number_of - 1)
    while rest > 0:
        candidates = [i for i in range(number_of - 1) if holding[i] < most]
        whole, left = sum([weights[i] for i in candidates]), rest
        for i in candidates:
            more = min(most - holding[i], max(1, left * weights[i] // whole), rest)
            holding[i] = holding[i] + more
            rest = rest - more
    return np.array([most] + holding)


def uneven_parts(key, count, total, most, skew):
    if count == 2:
        one = jax.random.randint(key, (), max(1, total - most), min(most, total - 1) + 1)
        return jnp.stack([one, total - one])
    sizes = jnp.asarray(split_up(count, total, most, skew), jnp.int32)
    couples = (count - 1) // 2
    giver, sink = sizes[1:1 + 2 * couples:2], sizes[2:2 + 2 * couples:2]
    room = jnp.minimum(giver - 1, most - sink)
    moved = jax.random.randint(jax.random.fold_in(key, 1), (couples,), 0, 1 << 20) % (room + 1)
    sizes = sizes.at[1:1 + 2 * couples:2].set(giver - moved).at[2:2 + 2 * couples:2].set(sink + moved)
    return sizes[jax.random.permutation(jax.random.fold_in(key, 2), count)]


def scatter_about(own_key, extent, scale, bound, shards=(), kind=jnp.bfloat16):
    drawn = scale * jax.random.normal(own_key, extent, jnp.float32)
    if shards:
        drawn = drawn * steps_of(own_key, extent, shards, -0.22, 0.18)
    return jnp.clip(drawn, -bound, bound).astype(kind)


def setup_inputs(seed: int = 0) -> dict:
    seeds = jax.random.split(jax.random.key(seed), 18)
    embedded = draw_embedded(jax.random.fold_in(seeds[17], 71), 0)
    cotangent = scatter_about(seeds[1], (TOKENS, D), 1.0, 6.0, ((0, 32),))
    doc_lengths = uneven_parts(seeds[2], NDOCS, TOKENS, DOC_MAX, 2).astype(jnp.int32)
    emb_gain = jnp.clip(1.0 + 0.15 * jax.random.normal(seeds[3], (D,), jnp.float32), 0.25, 1.75)
    emb_bias = scatter_about(seeds[4], (D,), 0.3, 3.0, (), jnp.float32)
    attn_gain = jnp.clip(1.0 + 0.15 * jax.random.normal(seeds[5], (LAYERS, D), jnp.float32), 0.25, 1.75)
    attn_bias = scatter_about(seeds[6], (LAYERS, D), 0.3, 3.0, (), jnp.float32)
    qkv_weight = scatter_about(seeds[7], (LAYERS, D, 3 * D), D ** -0.5, 0.125, ((1, 8), (2, 4)))
    qv_bias = scatter_about(seeds[8], (LAYERS, H, 2, HD), 0.5, 4.0, (), jnp.float32)
    out_weight = scatter_about(seeds[9], (LAYERS, D, D), (D // 16) ** -0.5, 0.5, ((1, 4), (2, 8)))
    out_bias = scatter_about(seeds[10], (LAYERS, D), 0.5, 4.0, (), jnp.float32)
    ffn_gain = jnp.clip(1.0 + 0.15 * jax.random.normal(seeds[11], (LAYERS, D), jnp.float32), 0.25, 1.75)
    ffn_bias = scatter_about(seeds[12], (LAYERS, D), 0.3, 3.0, (), jnp.float32)
    up_weight = scatter_about(seeds[13], (LAYERS, D, FF), D ** -0.5, 0.125, ((1, 8), (2, 4)))
    up_bias = scatter_about(seeds[14], (LAYERS, FF), 0.5, 4.0, (), jnp.float32)
    down_weight = scatter_about(seeds[15], (LAYERS, FF, D), FF ** -0.5, 0.0625, ((1, 4), (2, 8)))
    down_bias = scatter_about(seeds[16], (LAYERS, D), 0.5, 4.0, (), jnp.float32)
    return dict(embedded=embedded, cotangent=cotangent, doc_lengths=doc_lengths, emb_gain=emb_gain, emb_bias=emb_bias, attn_gain=attn_gain, attn_bias=attn_bias, qkv_weight=qkv_weight, qv_bias=qv_bias, out_weight=out_weight, out_bias=out_bias, ffn_gain=ffn_gain, ffn_bias=ffn_bias, up_weight=up_weight, up_bias=up_bias, down_weight=down_weight, down_bias=down_bias)


norm_eps = 1e-05
highest = lax.Precision.HIGHEST

@jax.custom_vjp
def low(v):
    return lax.optimization_barrier(v.astype(jnp.bfloat16)).astype(jnp.float32)

@jax.custom_vjp
def low_back(v):
    return v

def low_keep(v):
    return (low(v), None)

def low_pass(kept, grad):
    return (grad,)

def back_keep(v):
    return (v, None)

def back_low(kept, grad):
    return (low(grad),)
low.defvjp(low_keep, low_pass)
low_back.defvjp(back_keep, back_low)

def layer_norm(values, gain_row, shifts):
    average = lax.optimization_barrier(jnp.mean(values, axis=-1, keepdims=True))
    centered = values - average
    variance = lax.optimization_barrier(jnp.mean(centered * centered, axis=-1, keepdims=True))
    return centered * lax.rsqrt(variance + norm_eps) * gain_row + shifts

def gelu_tanh(values):
    return 0.5 * values * (1.0 + jnp.tanh(0.7978845608028654 * (values + 0.044715 * values * values * values)))

def rounded_both(values):
    return low_back(low(values))

def stream_attention(grouped, doc_ids):
    block_rows = min(512, TOKENS)
    window = min(TOKENS, DOC_MAX + block_rows)
    slopes = jnp.exp2(-8.0 * (jnp.arange(H) + 1).astype(jnp.float32) / H)
    scale_factor = HD ** (-0.5)

    def one_block(block_start):
        key_first = jnp.clip(block_start + block_rows - window, 0, TOKENS - window).astype(jnp.int32)
        queries = lax.dynamic_slice_in_dim(grouped, block_start, block_rows, 0)[:, :, 0]
        nearby = lax.dynamic_slice_in_dim(grouped, key_first, window, 0)
        key_rows = nearby[:, :, 1]
        value_rows = nearby[:, :, 2]
        query_pos = block_start + jnp.arange(block_rows, dtype=jnp.int32)
        key_pos = key_first + jnp.arange(window, dtype=jnp.int32)
        query_doc = lax.dynamic_slice_in_dim(doc_ids, block_start, block_rows, 0)
        key_doc = lax.dynamic_slice_in_dim(doc_ids, key_first, window, 0)
        raw_scores = jnp.einsum('qhd,khd->hqk', queries, key_rows, precision=highest) * scale_factor
        distance = (key_pos[None, :] - query_pos[:, None]).astype(jnp.float32)
        raw_scores = low_back(raw_scores + slopes[:, None, None] * distance[None, :, :])
        allowed = (key_pos[None, :] <= query_pos[:, None]) & (key_doc[None, :] == query_doc[:, None])
        attn_probs = jax.nn.softmax(jnp.where(allowed[None, :, :], raw_scores, -jnp.inf), axis=-1)
        return jnp.einsum('hqk,khd->qhd', low(attn_probs), value_rows, precision=highest)
    block_starts = (jnp.arange(TOKENS // block_rows) * block_rows).astype(jnp.int32)
    blocks_out = lax.map(jax.checkpoint(one_block), block_starts)
    return blocks_out.reshape(TOKENS, H, HD)

def block_layer(hidden, doc_ids, layer_args):
    attn_gain, attn_bias, qkv_weight, qv_bias, out_weight, out_bias, ffn_gain, ffn_bias, up_weight, up_bias, down_weight, down_bias = layer_args
    normed = low(layer_norm(hidden, attn_gain, attn_bias))
    bias_all = jnp.stack([qv_bias[:, 0], jnp.zeros_like(qv_bias[:, 0]), qv_bias[:, 1]], axis=1)
    projected = jnp.dot(normed, qkv_weight, precision=highest).reshape(TOKENS, H, 3, HD) + bias_all
    grouped = rounded_both(projected)
    context = rounded_both(stream_attention(grouped, doc_ids)).reshape(TOKENS, D)
    attn_out = low_back(jnp.dot(context, out_weight, precision=highest) + out_bias)
    hidden_mid = hidden + attn_out
    ffn_normed = low(layer_norm(hidden_mid, ffn_gain, ffn_bias))
    up_pre = low_back(jnp.dot(ffn_normed, up_weight, precision=highest) + up_bias)
    activated = low(gelu_tanh(up_pre))
    return hidden_mid + low_back(jnp.dot(activated, down_weight, precision=highest) + down_bias)

def reference(embedded, cotangent, doc_lengths, emb_gain, emb_bias, attn_gain, attn_bias, qkv_weight, qv_bias, out_weight, out_bias, ffn_gain, ffn_bias, up_weight, up_bias, down_weight, down_bias):
    lengths_int = doc_lengths.astype(jnp.int32)
    doc_starts = (jnp.cumsum(lengths_int) - lengths_int).astype(jnp.int32)
    positions = jnp.arange(TOKENS, dtype=jnp.int32)
    doc_ids = (lax.optimization_barrier(jnp.sum((positions[:, None] >= doc_starts[None, :]).astype(jnp.int32), axis=1)) - 1).astype(jnp.int32)
    params = (embedded.astype(jnp.float32), emb_gain, emb_bias, attn_gain, attn_bias, qkv_weight.astype(jnp.float32), qv_bias, out_weight.astype(jnp.float32), out_bias, ffn_gain, ffn_bias, up_weight.astype(jnp.float32), up_bias, down_weight.astype(jnp.float32), down_bias)

    def forward_stream(weights_all):
        hidden = layer_norm(weights_all[0], weights_all[1], weights_all[2])
        for layer_index in range(LAYERS):
            layer_args = tuple((member[layer_index] for member in weights_all[3:]))
            hidden = block_layer(hidden, doc_ids, layer_args)
        return hidden
    hidden_out, pullback = jax.vjp(forward_stream, params)
    grads = pullback(cotangent.astype(jnp.float32))[0]
    return (hidden_out, grads[0], grads[1], grads[2], grads[3], grads[4], grads[5], grads[6], grads[7], grads[8], grads[9], grads[10], grads[11], grads[12], grads[13], grads[14])
```

```python
from functools import partial

import jax
import jax.numpy as jnp
from jax import lax
from jax.experimental import pallas as pl
from jax.experimental.pallas import tpu as pltpu
from jax.sharding import PartitionSpec as P

D = 2048
H = 16
HD = 128
FF = 8192
LAYERS = 2

norm_eps = 1e-05
bf16 = jnp.bfloat16
f32 = jnp.float32


def layer_norm(values, gain_row, shifts):
    average = jnp.mean(values, axis=-1, keepdims=True)
    centered = values - average
    variance = jnp.mean(centered * centered, axis=-1, keepdims=True)
    return centered * lax.rsqrt(variance + norm_eps) * gain_row + shifts


def gelu_tanh(values):
    return (
        0.5
        * values
        * (1.0 + jnp.tanh(0.7978845608028654 * (values + 0.044715 * values * values * values)))
    )


def dot(left, right, left_dim, right_dim):
    return lax.dot_general(
        left, right, (((left_dim,), (right_dim,)), ((), ())), preferred_element_type=f32
    )


def ring_ok():
    return lax.axis_size("blk") == 8


def z_next(value, step):
    pairs = [(z * 2 + x, (z + step) % 4 * 2 + x) for z in range(4) for x in range(2)]
    return lax.ppermute(value, "blk", pairs)


def x_swap(value):
    return lax.ppermute(value, "blk", [(i, i ^ 1) for i in range(8)])


def to_relative(values):
    if not ring_ok():
        return values
    index = lax.axis_index("blk")
    z, x = index // 2, index % 2
    width = values.shape[-1] // 8
    parts = [values[..., i * width : (i + 1) * width] for i in range(8)]
    swapped = [parts[i ^ 1] for i in range(8)]
    mine = jnp.where(x == 0, jnp.concatenate(parts, -1), jnp.concatenate(swapped, -1))
    twice = jnp.concatenate([mine, mine], -1)
    return lax.dynamic_slice_in_dim(twice, z * 2 * width, 8 * width, values.ndim - 1)


def to_absolute(values):
    if not ring_ok():
        return values
    index = lax.axis_index("blk")
    z, x = index // 2, index % 2
    width = values.shape[-1] // 8
    twice = jnp.concatenate([values, values], -1)
    turned = lax.dynamic_slice_in_dim(twice, (4 - z) % 4 * 2 * width, 8 * width, values.ndim - 1)
    parts = [turned[..., i * width : (i + 1) * width] for i in range(8)]
    swapped = [parts[i ^ 1] for i in range(8)]
    return jnp.where(x == 0, turned, jnp.concatenate(swapped, -1))


def gather_blocks(shard, axis):
    if not ring_ok():
        return lax.all_gather(shard, "blk", axis=axis, tiled=True)
    held = [shard]
    for _ in range(3):
        held.append(z_next(held[-1], -1))
    pieces = []
    for piece in held:
        pieces += [piece, x_swap(piece)]
    return jnp.concatenate(pieces, axis)


def sum_blocks(piece_of, axis):
    if not ring_ok():
        whole = jnp.concatenate([piece_of(i) for i in range(lax.axis_size("blk"))], axis)
        return lax.psum_scatter(
            whole.astype(bf16), "blk", scatter_dimension=axis, tiled=True
        ).astype(f32)
    total = None
    for k in (3, 2, 1, 0):
        came = x_swap(piece_of(2 * k + 1).astype(bf16))
        mine = piece_of(2 * k).astype(f32) + came.astype(f32)
        if total is not None:
            mine = mine + total.astype(f32)
        if k > 0:
            total = z_next(mine.astype(bf16), 1)
    return mine


def butterfly(values, axis):
    distance = 1
    while distance < lax.axis_size(axis):
        pairs = [(i, i ^ distance) for i in range(lax.axis_size(axis))]
        values = values + lax.ppermute(values, axis, pairs)
        distance *= 2
    return values


def from_behind(block, distance):
    count = lax.axis_size("blk")
    return lax.ppermute(block, "blk", [(i, i + distance) for i in range(count - distance)])


def to_behind(block, distance):
    count = lax.axis_size("blk")
    return lax.ppermute(block, "blk", [(i + distance, i) for i in range(count - distance)])


def gather_rows(values):
    return lax.all_gather(values, "head", axis=0, tiled=True)


def sum_rows(values):
    return lax.psum_scatter(
        values.astype(bf16), "head", scatter_dimension=0, tiled=True
    ).astype(f32)


def key_parts(own_ref, near_ref, far_ref):
    keys = [far_ref[:, :HD], near_ref[:, :HD], own_ref[:, HD : 2 * HD]]
    values = [far_ref[:, HD:], near_ref[:, HD:], own_ref[:, 2 * HD :]]
    return keys, values


def softmax_parts(slope, start_row, queries, keys):
    rows = queries.shape[0]
    scale = HD ** (-0.5)
    query_at = lax.broadcasted_iota(jnp.int32, (rows, rows), 1)
    parts = []
    for i, key in enumerate(keys):
        key_at = lax.broadcasted_iota(jnp.int32, (rows, rows), 0) + (i - 2) * rows
        scores = dot(key, queries, 1, 1) * scale
        scores = scores + slope * (key_at - query_at).astype(f32)
        allowed = (key_at <= query_at) & (key_at >= start_row)
        parts.append(jnp.where(allowed, scores, -jnp.inf))
    top = jnp.maximum(
        jnp.maximum(jnp.max(parts[0], 0, keepdims=True), jnp.max(parts[1], 0, keepdims=True)),
        jnp.max(parts[2], 0, keepdims=True),
    )
    parts = [jnp.exp(part - top) for part in parts]
    total = sum(jnp.sum(part, 0, keepdims=True) for part in parts)
    share = 1.0 / total
    return [part * share for part in parts]


def attend_kernel(slope_ref, start_ref, own_ref, near_ref, far_ref, out_ref):
    slope = slope_ref[pl.program_id(0)]
    keys, values = key_parts(own_ref, near_ref, far_ref)
    probs = softmax_parts(slope, start_ref[0:1, :], own_ref[:, :HD], keys)
    out = sum(dot(p.astype(bf16), v, 0, 0) for p, v in zip(probs, values))
    out_ref[...] = out.astype(out_ref.dtype)


def attend_back_kernel(
    slope_ref, start_ref, own_ref, near_ref, far_ref, grad_ref, own_out, near_out, far_out
):
    slope = slope_ref[pl.program_id(0)]
    scale = HD ** (-0.5)
    keys, values = key_parts(own_ref, near_ref, far_ref)
    queries = own_ref[:, :HD]
    grad = grad_ref[...]
    probs = softmax_parts(slope, start_ref[0:1, :], queries, keys)
    back = [dot(v, grad, 1, 1) for v in values]
    delta = sum(jnp.sum(p * b, 0, keepdims=True) for p, b in zip(probs, back))
    score_grads = [(p * (b - delta)).astype(bf16) for p, b in zip(probs, back)]
    grad_q = sum(dot(s, k, 0, 0) for s, k in zip(score_grads, keys))
    grad_k = [dot(s, queries, 1, 0) * scale for s in score_grads]
    grad_v = [dot(p.astype(bf16), grad, 1, 0) for p in probs]
    far_out[:, :HD] = grad_k[0].astype(bf16)
    far_out[:, HD:] = grad_v[0].astype(bf16)
    near_out[:, :HD] = grad_k[1].astype(bf16)
    near_out[:, HD:] = grad_v[1].astype(bf16)
    own_out[:, :HD] = grad_q * scale
    own_out[:, HD : 2 * HD] = grad_k[2]
    own_out[:, 2 * HD :] = grad_v[2]


def join_kernel(own_ref, near_ref, far_ref, out_ref):
    out_ref[:, :HD] = own_ref[:, :HD].astype(bf16)
    both = own_ref[:, HD:] + (near_ref[...].astype(f32) + far_ref[...].astype(f32))
    out_ref[:, HD:] = both.astype(bf16)


def head_block(rows, width):
    return pl.BlockSpec((rows, width), lambda h: (0, h))


def attention_specs(rows):
    return [
        pl.BlockSpec(memory_space=pltpu.SMEM),
        pl.BlockSpec((8, rows), lambda h: (0, 0)),
        head_block(rows, 3 * HD),
        head_block(rows, 2 * HD),
        head_block(rows, 2 * HD),
    ]


def attend(slopes, start_rows, own, near, far):
    rows, heads = own.shape[0], own.shape[1] // (3 * HD)
    return pl.pallas_call(
        attend_kernel,
        grid=(heads,),
        in_specs=attention_specs(rows),
        out_specs=head_block(rows, HD),
        out_shape=jax.ShapeDtypeStruct((rows, heads * HD), bf16),
        cost_estimate=pl.CostEstimate(
            flops=heads * 12 * rows * rows * HD,
            bytes_accessed=rows * heads * HD * 16,
            transcendentals=heads * 3 * rows * rows,
        ),
        name="attend",
    )(slopes, start_rows, own, near, far)


def attend_back(slopes, start_rows, own, near, far, grad):
    rows, heads = own.shape[0], own.shape[1] // (3 * HD)
    return pl.pallas_call(
        attend_back_kernel,
        grid=(heads,),
        in_specs=attention_specs(rows) + [head_block(rows, HD)],
        out_specs=[head_block(rows, 3 * HD), head_block(rows, 2 * HD), head_block(rows, 2 * HD)],
        out_shape=[
            jax.ShapeDtypeStruct((rows, heads * 3 * HD), f32),
            jax.ShapeDtypeStruct((rows, heads * 2 * HD), bf16),
            jax.ShapeDtypeStruct((rows, heads * 2 * HD), bf16),
        ],
        cost_estimate=pl.CostEstimate(
            flops=heads * 30 * rows * rows * HD,
            bytes_accessed=rows * heads * HD * 32,
            transcendentals=heads * 3 * rows * rows,
        ),
        name="attend_back",
    )(slopes, start_rows, own, near, far, grad)


def join_grads(own, near, far):
    rows, heads = own.shape[0], own.shape[1] // (3 * HD)
    return pl.pallas_call(
        join_kernel,
        grid=(heads,),
        in_specs=[head_block(rows, 3 * HD), head_block(rows, 2 * HD), head_block(rows, 2 * HD)],
        out_specs=head_block(rows, 3 * HD),
        out_shape=jax.ShapeDtypeStruct(own.shape, bf16),
        cost_estimate=pl.CostEstimate(
            flops=own.size * 2, bytes_accessed=own.size * 9, transcendentals=0
        ),
        name="join_grads",
    )(own, near, far)


def body(
    embedded,
    cotangent,
    doc_lengths,
    emb_gain,
    emb_bias,
    attn_gain,
    attn_bias,
    qkv_weight,
    qv_bias,
    out_weight,
    out_bias,
    ffn_gain,
    ffn_bias,
    up_weight,
    up_bias,
    down_weight,
    down_bias,
):
    head_count = lax.axis_size("head")
    head_index = lax.axis_index("head")
    blk_index = lax.axis_index("blk")
    group_rows = embedded.shape[0] * head_count
    heads_local = H // head_count
    ff_local = FF // head_count
    block = D // lax.axis_size("blk")

    doc_starts = jnp.cumsum(doc_lengths) - doc_lengths
    query_pos = blk_index * group_rows + jnp.arange(group_rows, dtype=jnp.int32)
    begun = doc_starts[None, :] <= query_pos[:, None]
    own_start = jnp.max(jnp.where(begun, doc_starts[None, :], 0), axis=1)
    start_rows = jnp.broadcast_to(
        (own_start - blk_index * group_rows).astype(jnp.int32)[None, :], (8, group_rows)
    )
    head_ids = head_index * heads_local + jnp.arange(heads_local)
    slopes = jnp.exp2(-8.0 * (head_ids + 1).astype(f32) / H)

    matrices = []
    for layer in range(LAYERS):
        matrices.append(
            (
                gather_blocks(qkv_weight[layer], 0),
                gather_blocks(out_weight[layer], 1),
                gather_blocks(up_weight[layer], 0),
                gather_blocks(down_weight[layer], 1),
            )
        )

    rows_in = jnp.stack([emb_gain, emb_bias])
    vectors = to_relative(
        jnp.concatenate(
            [rows_in, attn_gain, attn_bias, out_bias, ffn_gain, ffn_bias, down_bias], axis=0
        )
    )
    emb_gain, emb_bias = vectors[0], vectors[1]
    attn_gain, attn_bias, out_bias, ffn_gain, ffn_bias, down_bias = (
        vectors[2 + LAYERS * i : 2 + LAYERS * (i + 1)] for i in range(6)
    )
    embedded_wide = to_relative(embedded).astype(f32)
    grad_now = to_relative(cotangent).astype(f32)

    hidden = layer_norm(embedded_wide, emb_gain, emb_bias)
    kept_values = []
    for layer in range(LAYERS):
        qkv_mat, out_mat, up_mat, down_mat = matrices[layer]
        zeros = jnp.zeros_like(qv_bias[layer][:, 0])
        bias_all = jnp.stack([qv_bias[layer][:, 0], zeros, qv_bias[layer][:, 1]], axis=1)
        own_bias = lax.dynamic_slice_in_dim(
            bias_all.reshape(-1), head_index * heads_local * 3 * HD, heads_local * 3 * HD, 0
        )
        normed = layer_norm(hidden, attn_gain[layer], attn_bias[layer]).astype(bf16)
        normed_rows = gather_rows(normed)
        own = (dot(normed_rows, qkv_mat, 1, 0) + own_bias).astype(bf16)
        sent = jnp.concatenate(
            [own[:, (3 * h + 1) * HD : (3 * h + 3) * HD] for h in range(heads_local)], axis=1
        )
        near, far = from_behind(sent, 1), from_behind(sent, 2)
        context = attend(slopes, start_rows, own, near, far)
        attn_out = sum_rows(dot(context, out_mat, 1, 0))
        hidden_mid = hidden + (attn_out + out_bias[layer])
        ffn_normed = layer_norm(hidden_mid, ffn_gain[layer], ffn_bias[layer]).astype(bf16)
        ffn_rows = gather_rows(ffn_normed)
        own_up_bias = lax.dynamic_slice_in_dim(up_bias[layer], head_index * ff_local, ff_local, 0)
        up_pre = dot(ffn_rows, up_mat, 1, 0) + own_up_bias
        activated = gelu_tanh(up_pre).astype(bf16)
        ffn_out = sum_rows(dot(activated, down_mat, 1, 0))
        kept_values.append(
            (hidden, hidden_mid, normed_rows, own, near, far, context, ffn_rows, up_pre, activated)
        )
        hidden = hidden_mid + (ffn_out + down_bias[layer])

    collected = [None] * LAYERS
    summed = [None] * LAYERS
    for layer in reversed(range(LAYERS)):
        qkv_mat, out_mat, up_mat, down_mat = matrices[layer]
        (layer_input, hidden_mid, normed_rows, own, near, far, context, ffn_rows, up_pre, activated) = (
            kept_values[layer]
        )
        cols = lambda values, i: values[:, i * block : (i + 1) * block]
        grad_low = grad_now.astype(bf16)
        down_bias_grad = jnp.sum(grad_low.astype(f32), axis=0)
        grad_rows = gather_rows(grad_low)
        grad_act = dot(grad_rows, down_mat, 1, 1)
        down_grad = sum_blocks(lambda i: dot(activated, cols(grad_rows, i), 0, 0), 1)
        grad_up = jax.vjp(gelu_tanh, up_pre)[1](grad_act)[0].astype(bf16)
        up_bias_grad = jnp.sum(grad_up.astype(f32), axis=0)
        up_grad = sum_blocks(lambda i: dot(cols(ffn_rows, i), grad_up, 0, 0), 0)
        grad_ffn_normed = sum_rows(dot(grad_up, up_mat, 1, 1))
        ffn_back = jax.vjp(layer_norm, hidden_mid, ffn_gain[layer], ffn_bias[layer])[1]
        grad_mid_part, ffn_gain_grad, ffn_bias_grad = ffn_back(grad_ffn_normed)
        grad_mid = grad_now + grad_mid_part
        attn_low = grad_mid.astype(bf16)
        out_bias_grad = jnp.sum(attn_low.astype(f32), axis=0)
        attn_grad_rows = gather_rows(attn_low)
        grad_context = dot(attn_grad_rows, out_mat, 1, 1).astype(bf16)
        out_grad = sum_blocks(lambda i: dot(context, cols(attn_grad_rows, i), 0, 0), 1)
        own_grad, near_grad, far_grad = attend_back(
            slopes, start_rows, own, near, far, grad_context
        )
        grad_qkv = join_grads(own_grad, to_behind(near_grad, 1), to_behind(far_grad, 2))
        qkv_bias_grad = jnp.sum(grad_qkv.astype(f32), axis=0)
        qkv_grad = sum_blocks(lambda i: dot(cols(normed_rows, i), grad_qkv, 0, 0), 0)
        grad_normed = sum_rows(dot(grad_qkv, qkv_mat, 1, 1))
        attn_back = jax.vjp(layer_norm, layer_input, attn_gain[layer], attn_bias[layer])[1]
        grad_in_part, attn_gain_grad, attn_bias_grad = attn_back(grad_normed)
        grad_now = grad_mid + grad_in_part
        collected[layer] = (qkv_grad, out_grad, up_grad, down_grad)
        common = [
            attn_gain_grad,
            attn_bias_grad,
            out_bias_grad,
            ffn_gain_grad,
            ffn_bias_grad,
            down_bias_grad,
        ]
        if layer == 0:
            emb_back = jax.vjp(layer_norm, embedded_wide, emb_gain, emb_bias)[1]
            embedded_grad, emb_gain_grad, emb_bias_grad = emb_back(grad_now)
            common += [emb_gain_grad, emb_bias_grad]
        common = to_absolute(jnp.stack(common))
        lone = jnp.concatenate([up_bias_grad, qkv_bias_grad])
        count = common.size
        flat = butterfly(jnp.concatenate([common.reshape(-1), lone]), "blk")
        common, lone = flat[:count], flat[count:]
        spread = lax.dynamic_update_slice_in_dim(
            jnp.zeros((lone.size * head_count,), f32), lone, head_index * lone.size, 0
        )
        flat = butterfly(jnp.concatenate([common, spread]), "head")
        common, lone = flat[:count].reshape(-1, D), flat[count:].reshape(head_count, -1)
        bias_sums = lone[:, ff_local:].reshape(H, 3, HD)
        summed[layer] = (
            common,
            lone[:, :ff_local].reshape(-1),
            jnp.stack([bias_sums[:, 0], bias_sums[:, 2]], axis=1),
        )

    def stacked(member):
        return jnp.stack([collected[layer][member] for layer in range(LAYERS)])

    def small(row):
        return jnp.stack([summed[layer][0][row] for layer in range(LAYERS)])

    return (
        to_absolute(hidden),
        to_absolute(embedded_grad),
        summed[0][0][6],
        summed[0][0][7],
        small(0),
        small(1),
        stacked(0),
        jnp.stack([summed[layer][2] for layer in range(LAYERS)]),
        stacked(1),
        small(2),
        small(3),
        small(4),
        stacked(2),
        jnp.stack([summed[layer][1] for layer in range(LAYERS)]),
        stacked(3),
        small(5),
    )


def solution(mesh):
    rows = P(("blk", "head"), None)
    tall, wide = P(None, "blk", "head"), P(None, "head", "blk")
    none = P()
    in_specs = (
        (rows, rows) + (none,) * 5 + (tall, none, wide, none, none, none, tall, none, wide, none)
    )
    out_specs = (
        (rows, rows) + (none,) * 4 + (tall, none, wide, none, none, none, tall, none, wide, none)
    )
    return jax.shard_map(body, mesh=mesh, in_specs=in_specs, out_specs=out_specs, check_vma=False)
```

```python
import jax
import jax.numpy as jnp
from jax import lax
from jax.experimental import pallas as pl
from jax.experimental.pallas import tpu as pltpu
from jax.sharding import PartitionSpec as P


D = 2048
H = 16
HD = 128
FF = 8192
LAYERS = 2

norm_eps = 1e-05
bf16 = jnp.bfloat16
f32 = jnp.float32


def layer_norm(values, gain_row, shifts):
    average = jnp.mean(values, axis=-1, keepdims=True)
    centered = values - average
    variance = jnp.mean(centered * centered, axis=-1, keepdims=True)
    return centered * lax.rsqrt(variance + norm_eps) * gain_row + shifts


def gelu_tanh(values):
    return (
        0.5
        * values
        * (1.0 + jnp.tanh(0.7978845608028654 * (values + 0.044715 * values * values * values)))
    )


def dot(left, right, left_dim, right_dim):
    return lax.dot_general(
        left, right, (((left_dim,), (right_dim,)), ((), ())), preferred_element_type=f32
    )


def ring_ok():
    return lax.axis_size("blk") == 8


def z_next(value, step):
    pairs = [(z * 2 + x, (z + step) % 4 * 2 + x) for z in range(4) for x in range(2)]
    return lax.ppermute(value, "blk", pairs)


def x_swap(value):
    return lax.ppermute(value, "blk", [(i, i ^ 1) for i in range(8)])


def to_relative(values):
    if not ring_ok():
        return values
    index = lax.axis_index("blk")
    z, x = index // 2, index % 2
    width = values.shape[-1] // 8
    parts = [values[..., i * width : (i + 1) * width] for i in range(8)]
    swapped = [parts[i ^ 1] for i in range(8)]
    mine = jnp.where(x == 0, jnp.concatenate(parts, -1), jnp.concatenate(swapped, -1))
    twice = jnp.concatenate([mine, mine], -1)
    return lax.dynamic_slice_in_dim(twice, z * 2 * width, 8 * width, values.ndim - 1)


def to_absolute(values):
    if not ring_ok():
        return values
    index = lax.axis_index("blk")
    z, x = index // 2, index % 2
    width = values.shape[-1] // 8
    twice = jnp.concatenate([values, values], -1)
    turned = lax.dynamic_slice_in_dim(twice, (4 - z) % 4 * 2 * width, 8 * width, values.ndim - 1)
    parts = [turned[..., i * width : (i + 1) * width] for i in range(8)]
    swapped = [parts[i ^ 1] for i in range(8)]
    return jnp.where(x == 0, turned, jnp.concatenate(swapped, -1))


BALANCED = ("q", "u")


def gather_blocks(shard, axis, tag):
    if not ring_ok():
        return lax.all_gather(shard, "blk", axis=axis, tiled=True)
    held = [shard]
    for _ in range(1, 4):
        held.append(z_next(held[-1], -1))
    across = [x_swap(held[k]) for k in range(3)]
    if tag[-1] in BALANCED:
        across.append(z_next(across[0], 1))
    else:
        across.append(x_swap(held[3]))
    return jnp.concatenate([p for pair in zip(held, across) for p in pair], axis)


def sum_blocks(piece_of, axis, tag):
    if not ring_ok():
        whole = jnp.concatenate([piece_of(i) for i in range(lax.axis_size("blk"))], axis)
        return lax.psum_scatter(
            whole.astype(bf16), "blk", scatter_dimension=axis, tiled=True
        ).astype(f32)
    balanced = tag[-1] in BALANCED
    total = aside = None
    for k in (3, 2, 1, 0):
        mine, other = piece_of(2 * k), piece_of(2 * k + 1)
        if balanced and k == 3:
            aside = z_next(other.astype(bf16), -1)
        else:
            if balanced and k == 0:
                other = other + aside.astype(f32)
            mine = mine + x_swap(other.astype(bf16)).astype(f32)
        if total is not None:
            mine = mine + total.astype(f32)
        if k > 0:
            total = z_next(mine.astype(bf16), 1)
    return mine


def butterfly(values, axis):
    distance = 1
    while distance < lax.axis_size(axis):
        pairs = [(i, i ^ distance) for i in range(lax.axis_size(axis))]
        values = values + lax.ppermute(values, axis, pairs)
        distance *= 2
    return values


def from_behind(block, distance):
    count = lax.axis_size("blk")
    return lax.ppermute(block, "blk", [(i, i + distance) for i in range(count - distance)])


def to_behind(block, distance):
    count = lax.axis_size("blk")
    return lax.ppermute(block, "blk", [(i + distance, i) for i in range(count - distance)])


def gather_rows(values):
    return lax.all_gather(values, "head", axis=0, tiled=True)


def sum_rows(values):
    return lax.psum_scatter(
        values.astype(bf16), "head", scatter_dimension=0, tiled=True
    ).astype(f32)


def key_parts(own_ref, near_ref, far_ref):
    keys = [far_ref[:, :HD], near_ref[:, :HD], own_ref[:, HD : 2 * HD]]
    values = [far_ref[:, HD:], near_ref[:, HD:], own_ref[:, 2 * HD :]]
    return keys, values


def softmax_parts(slope, start_row, queries, keys):
    rows = queries.shape[0]
    scale = HD ** (-0.5)
    query_at = lax.broadcasted_iota(jnp.int32, (rows, rows), 1)
    parts = []
    for i, key in enumerate(keys):
        key_at = lax.broadcasted_iota(jnp.int32, (rows, rows), 0) + (i - 2) * rows
        scores = dot(key, queries, 1, 1) * scale
        scores = scores + slope * (key_at - query_at).astype(f32)
        allowed = (key_at <= query_at) & (key_at >= start_row)
        parts.append(jnp.where(allowed, scores, -jnp.inf))
    top = jnp.maximum(
        jnp.maximum(jnp.max(parts[0], 0, keepdims=True), jnp.max(parts[1], 0, keepdims=True)),
        jnp.max(parts[2], 0, keepdims=True),
    )
    parts = [jnp.exp(part - top) for part in parts]
    total = sum(jnp.sum(part, 0, keepdims=True) for part in parts)
    share = 1.0 / total
    return [part * share for part in parts]


def attend_kernel(slope_ref, start_ref, own_ref, near_ref, far_ref, out_ref):
    slope = slope_ref[pl.program_id(0)]
    keys, values = key_parts(own_ref, near_ref, far_ref)
    probs = softmax_parts(slope, start_ref[0:1, :], own_ref[:, :HD], keys)
    out = sum(dot(p.astype(bf16), v, 0, 0) for p, v in zip(probs, values))
    out_ref[...] = out.astype(out_ref.dtype)


def attend_back_kernel(
    slope_ref, start_ref, own_ref, near_ref, far_ref, grad_ref, own_out, near_out, far_out
):
    slope = slope_ref[pl.program_id(0)]
    scale = HD ** (-0.5)
    keys, values = key_parts(own_ref, near_ref, far_ref)
    queries = own_ref[:, :HD]
    grad = grad_ref[...]
    probs = softmax_parts(slope, start_ref[0:1, :], queries, keys)
    back = [dot(v, grad, 1, 1) for v in values]
    delta = sum(jnp.sum(p * b, 0, keepdims=True) for p, b in zip(probs, back))
    score_grads = [(p * (b - delta)).astype(bf16) for p, b in zip(probs, back)]
    grad_q = sum(dot(s, k, 0, 0) for s, k in zip(score_grads, keys))
    grad_k = [dot(s, queries, 1, 0) * scale for s in score_grads]
    grad_v = [dot(p.astype(bf16), grad, 1, 0) for p in probs]
    far_out[:, :HD] = grad_k[0].astype(bf16)
    far_out[:, HD:] = grad_v[0].astype(bf16)
    near_out[:, :HD] = grad_k[1].astype(bf16)
    near_out[:, HD:] = grad_v[1].astype(bf16)
    own_out[:, :HD] = grad_q * scale
    own_out[:, HD : 2 * HD] = grad_k[2]
    own_out[:, 2 * HD :] = grad_v[2]


def join_kernel(own_ref, near_ref, far_ref, out_ref):
    out_ref[:, :HD] = own_ref[:, :HD].astype(bf16)
    both = own_ref[:, HD:] + (near_ref[...].astype(f32) + far_ref[...].astype(f32))
    out_ref[:, HD:] = both.astype(bf16)


def head_block(rows, width):
    return pl.BlockSpec((rows, width), lambda h: (0, h))


def attention_specs(rows):
    return [
        pl.BlockSpec(memory_space=pltpu.SMEM),
        pl.BlockSpec((8, rows), lambda h: (0, 0)),
        head_block(rows, 3 * HD),
        head_block(rows, 2 * HD),
        head_block(rows, 2 * HD),
    ]


def attend(slopes, start_rows, own, near, far):
    rows, heads = own.shape[0], own.shape[1] // (3 * HD)
    return pl.pallas_call(
        attend_kernel,
        grid=(heads,),
        in_specs=attention_specs(rows),
        out_specs=head_block(rows, HD),
        out_shape=jax.ShapeDtypeStruct((rows, heads * HD), bf16),
        cost_estimate=pl.CostEstimate(
            flops=heads * 12 * rows * rows * HD,
            bytes_accessed=rows * heads * HD * 16,
            transcendentals=heads * 3 * rows * rows,
        ),
        name="attend",
    )(slopes, start_rows, own, near, far)


def attend_back(slopes, start_rows, own, near, far, grad):
    rows, heads = own.shape[0], own.shape[1] // (3 * HD)
    return pl.pallas_call(
        attend_back_kernel,
        grid=(heads,),
        in_specs=attention_specs(rows) + [head_block(rows, HD)],
        out_specs=[head_block(rows, 3 * HD), head_block(rows, 2 * HD), head_block(rows, 2 * HD)],
        out_shape=[
            jax.ShapeDtypeStruct((rows, heads * 3 * HD), f32),
            jax.ShapeDtypeStruct((rows, heads * 2 * HD), bf16),
            jax.ShapeDtypeStruct((rows, heads * 2 * HD), bf16),
        ],
        cost_estimate=pl.CostEstimate(
            flops=heads * 30 * rows * rows * HD,
            bytes_accessed=rows * heads * HD * 32,
            transcendentals=heads * 3 * rows * rows,
        ),
        name="attend_back",
    )(slopes, start_rows, own, near, far, grad)


def join_grads(own, near, far):
    rows, heads = own.shape[0], own.shape[1] // (3 * HD)
    return pl.pallas_call(
        join_kernel,
        grid=(heads,),
        in_specs=[head_block(rows, 3 * HD), head_block(rows, 2 * HD), head_block(rows, 2 * HD)],
        out_specs=head_block(rows, 3 * HD),
        out_shape=jax.ShapeDtypeStruct(own.shape, bf16),
        cost_estimate=pl.CostEstimate(
            flops=own.size * 2, bytes_accessed=own.size * 9, transcendentals=0
        ),
        name="join_grads",
    )(own, near, far)


def program(
    embedded,
    cotangent,
    doc_lengths,
    emb_gain,
    emb_bias,
    attn_gain,
    attn_bias,
    qkv_weight,
    qv_bias,
    out_weight,
    out_bias,
    ffn_gain,
    ffn_bias,
    up_weight,
    up_bias,
    down_weight,
    down_bias,
):
    head_count = lax.axis_size("head")
    head_index = lax.axis_index("head")
    blk_index = lax.axis_index("blk")
    group_rows = embedded.shape[0] * head_count
    heads_local = H // head_count
    ff_local = FF // head_count
    block = D // lax.axis_size("blk")

    doc_starts = jnp.cumsum(doc_lengths) - doc_lengths
    query_pos = blk_index * group_rows + jnp.arange(group_rows, dtype=jnp.int32)
    begun = doc_starts[None, :] <= query_pos[:, None]
    own_start = jnp.max(jnp.where(begun, doc_starts[None, :], 0), axis=1)
    start_rows = jnp.broadcast_to(
        (own_start - blk_index * group_rows).astype(jnp.int32)[None, :], (8, group_rows)
    )
    head_ids = head_index * heads_local + jnp.arange(heads_local)
    slopes = jnp.exp2(-8.0 * (head_ids + 1).astype(f32) / H)

    matrices = []
    for layer in range(LAYERS):
        matrices.append(
            (
                gather_blocks(qkv_weight[layer], 0, f"{layer}q"),
                gather_blocks(out_weight[layer], 1, f"{layer}o"),
                gather_blocks(up_weight[layer], 0, f"{layer}u"),
                gather_blocks(down_weight[layer], 1, f"{layer}d"),
            )
        )

    rows_in = jnp.stack([emb_gain, emb_bias])
    vectors = to_relative(
        jnp.concatenate(
            [rows_in, attn_gain, attn_bias, out_bias, ffn_gain, ffn_bias, down_bias], axis=0
        )
    )
    emb_gain, emb_bias = vectors[0], vectors[1]
    attn_gain, attn_bias, out_bias, ffn_gain, ffn_bias, down_bias = (
        vectors[2 + LAYERS * i : 2 + LAYERS * (i + 1)] for i in range(6)
    )
    embedded_wide = to_relative(embedded).astype(f32)
    grad_now = to_relative(cotangent).astype(f32)

    hidden = layer_norm(embedded_wide, emb_gain, emb_bias)
    kept_values = []
    for layer in range(LAYERS):
        qkv_mat, out_mat, up_mat, down_mat = matrices[layer]
        zeros = jnp.zeros_like(qv_bias[layer][:, 0])
        bias_all = jnp.stack([qv_bias[layer][:, 0], zeros, qv_bias[layer][:, 1]], axis=1)
        own_bias = lax.dynamic_slice_in_dim(
            bias_all.reshape(-1), head_index * heads_local * 3 * HD, heads_local * 3 * HD, 0
        )
        normed = layer_norm(hidden, attn_gain[layer], attn_bias[layer]).astype(bf16)
        normed_rows = gather_rows(normed)
        own = (dot(normed_rows, qkv_mat, 1, 0) + own_bias).astype(bf16)
        sent = jnp.concatenate(
            [own[:, (3 * h + 1) * HD : (3 * h + 3) * HD] for h in range(heads_local)], axis=1
        )
        near, far = from_behind(sent, 1), from_behind(sent, 2)
        context = attend(slopes, start_rows, own, near, far)
        attn_out = sum_rows(dot(context, out_mat, 1, 0))
        hidden_mid = hidden + (attn_out + out_bias[layer])
        ffn_normed = layer_norm(hidden_mid, ffn_gain[layer], ffn_bias[layer]).astype(bf16)
        ffn_rows = gather_rows(ffn_normed)
        own_up_bias = lax.dynamic_slice_in_dim(up_bias[layer], head_index * ff_local, ff_local, 0)
        up_pre = dot(ffn_rows, up_mat, 1, 0) + own_up_bias
        activated = gelu_tanh(up_pre).astype(bf16)
        ffn_out = sum_rows(dot(activated, down_mat, 1, 0))
        kept_values.append(
            (hidden, hidden_mid, normed_rows, own, near, far, context, ffn_rows, up_pre, activated)
        )
        hidden = hidden_mid + (ffn_out + down_bias[layer])

    collected = [None] * LAYERS
    summed = [None] * LAYERS
    for layer in reversed(range(LAYERS)):
        qkv_mat, out_mat, up_mat, down_mat = matrices[layer]
        (layer_input, hidden_mid, normed_rows, own, near, far, context, ffn_rows, up_pre, activated) = (
            kept_values[layer]
        )
        cols = lambda values, i: values[:, i * block : (i + 1) * block]
        grad_low = grad_now.astype(bf16)
        down_bias_grad = jnp.sum(grad_low.astype(f32), axis=0)
        grad_rows = gather_rows(grad_low)
        grad_act = dot(grad_rows, down_mat, 1, 1)
        down_grad = sum_blocks(lambda i: dot(activated, cols(grad_rows, i), 0, 0), 1, f"{layer}d")
        grad_up = jax.vjp(gelu_tanh, up_pre)[1](grad_act)[0].astype(bf16)
        up_bias_grad = jnp.sum(grad_up.astype(f32), axis=0)
        up_grad = sum_blocks(lambda i: dot(cols(ffn_rows, i), grad_up, 0, 0), 0, f"{layer}u")
        grad_ffn_normed = sum_rows(dot(grad_up, up_mat, 1, 1))
        ffn_back = jax.vjp(layer_norm, hidden_mid, ffn_gain[layer], ffn_bias[layer])[1]
        grad_mid_part, ffn_gain_grad, ffn_bias_grad = ffn_back(grad_ffn_normed)
        grad_mid = grad_now + grad_mid_part
        attn_low = grad_mid.astype(bf16)
        out_bias_grad = jnp.sum(attn_low.astype(f32), axis=0)
        attn_grad_rows = gather_rows(attn_low)
        grad_context = dot(attn_grad_rows, out_mat, 1, 1).astype(bf16)
        out_grad = sum_blocks(lambda i: dot(context, cols(attn_grad_rows, i), 0, 0), 1, f"{layer}o")
        own_grad, near_grad, far_grad = attend_back(
            slopes, start_rows, own, near, far, grad_context
        )
        grad_qkv = join_grads(own_grad, to_behind(near_grad, 1), to_behind(far_grad, 2))
        qkv_bias_grad = jnp.sum(grad_qkv.astype(f32), axis=0)
        qkv_grad = sum_blocks(lambda i: dot(cols(normed_rows, i), grad_qkv, 0, 0), 0, f"{layer}q")
        grad_normed = sum_rows(dot(grad_qkv, qkv_mat, 1, 1))
        attn_back = jax.vjp(layer_norm, layer_input, attn_gain[layer], attn_bias[layer])[1]
        grad_in_part, attn_gain_grad, attn_bias_grad = attn_back(grad_normed)
        grad_now = grad_mid + grad_in_part
        collected[layer] = (qkv_grad, out_grad, up_grad, down_grad)
        common = [
            attn_gain_grad,
            attn_bias_grad,
            out_bias_grad,
            ffn_gain_grad,
            ffn_bias_grad,
            down_bias_grad,
        ]
        if layer == 0:
            emb_back = jax.vjp(layer_norm, embedded_wide, emb_gain, emb_bias)[1]
            embedded_grad, emb_gain_grad, emb_bias_grad = emb_back(grad_now)
            common += [emb_gain_grad, emb_bias_grad]
        common = to_absolute(jnp.stack(common))
        lone = jnp.concatenate([up_bias_grad, qkv_bias_grad])
        count = common.size
        flat = butterfly(jnp.concatenate([common.reshape(-1), lone]), "blk")
        common, lone = flat[:count], flat[count:]
        spread = lax.dynamic_update_slice_in_dim(
            jnp.zeros((lone.size * head_count,), f32), lone, head_index * lone.size, 0
        )
        flat = butterfly(jnp.concatenate([common, spread]), "head")
        common, lone = flat[:count].reshape(-1, D), flat[count:].reshape(head_count, -1)
        bias_sums = lone[:, ff_local:].reshape(H, 3, HD)
        summed[layer] = (
            common,
            lone[:, :ff_local].reshape(-1),
            jnp.stack([bias_sums[:, 0], bias_sums[:, 2]], axis=1),
        )

    def stacked(member):
        return jnp.stack([collected[layer][member] for layer in range(LAYERS)])

    def small(row):
        return jnp.stack([summed[layer][0][row] for layer in range(LAYERS)])

    return (
        to_absolute(hidden),
        to_absolute(embedded_grad),
        summed[0][0][6],
        summed[0][0][7],
        small(0),
        small(1),
        stacked(0),
        jnp.stack([summed[layer][2] for layer in range(LAYERS)]),
        stacked(1),
        small(2),
        small(3),
        small(4),
        stacked(2),
        jnp.stack([summed[layer][1] for layer in range(LAYERS)]),
        stacked(3),
        small(5),
    )


def solution(mesh):
    rows = P(("blk", "head"), None)
    tall, wide = P(None, "blk", "head"), P(None, "head", "blk")
    none = P()
    in_specs = (
        (rows, rows) + (none,) * 5 + (tall, none, wide, none, none, none, tall, none, wide, none)
    )
    out_specs = (
        (rows, rows) + (none,) * 4 + (tall, none, wide, none, none, none, tall, none, wide, none)
    )
    return jax.shard_map(program, mesh=mesh, in_specs=in_specs, out_specs=out_specs, check_vma=False)
```
